256 devices in a mesh: energy: 64 (over x, y, z_lo, core), dom: 4 (over z_hi).
Axes of the slice: x: 4, y: 4, z: 8 (z_hi: 4, z_lo: 2; z = z_hi * 2 + z_lo), core: 2. Of those that a mesh axis runs over, the one named last changes fastest.
Arguments:
- pivots: float32 [64, 32, 320, 320], P('energy', 'dom'), may hold values from -0.0125 to 1.4125
- lower_spikes: float32 [64, 32, 320, 320], P('energy', 'dom'), may hold values from -0.0125 to 1.0025
- upper_spikes: float32 [64, 32, 320, 320], P('energy', 'dom'), may hold values from -0.0125 to 1.0025
- potential: float32 [32, 320, 320], P('dom', 'energy'), may hold values from -0.3125 to 0.3125
- grain_of_slice: int32 [32], P('dom'), may hold values from 0 to 31
- grain_shift: float32 [32], replicated, may hold values from 0.5 to 1.5
- probes: float32 [32, 320, 128], P('dom'), may hold values from -6 to 6
- weights: float32 [64], P('energy'), may hold values from 0.5 to 2
Outputs:
- response: float32 [32, 320], P('dom', 'energy')
The draws below stay inside these ranges and needn't reach their ends.
All inputs are finite; a program needn't handle non-finite values.
Results may differ from the reference program's by a relative error of at most 0.00021.
Values sent between devices are 32-bit elements; how exact they have to be, the bound alone decides.
A program may use at most 128 MiB of HBM per device.

```python
import math
import jax
import jax.numpy as jnp
from jax import lax

B = 320
PROBES = 128
GRAINS = 32
SLICES = 32
ENERGIES = 64


def make_blocks(key, lower_end, upper_end):
    diag_key, noise_key = jax.random.split(key)
    diagonal = jax.random.uniform(diag_key, (ENERGIES, SLICES, B), jnp.float32, lower_end, upper_end)
    noise_part = jnp.clip(jax.random.normal(noise_key, (ENERGIES, SLICES, B, B), jnp.float32), -4.0, 4.0)
    return noise_part * (1.0 / B) + diagonal[..., None] * jnp.eye(B, dtype=jnp.float32)


def draw_pivots(key, part):
    return make_blocks(jax.random.fold_in(key, 11), 0.6, 1.3)


def draw_lower_spikes(key, part):
    return make_blocks(jax.random.fold_in(key, 23), 0.9, 0.98)


def draw_upper_spikes(key, part):
    return make_blocks(jax.random.fold_in(key, 37), 0.9, 0.98)


def place_ends(entries, key, least, largest):
    longest = entries.shape.index(max(entries.shape))
    spots = []
    for shift in (0, 1):
        where = [jax.random.randint(jax.random.fold_in(key, axis), (), 0, length) for axis, length in enumerate(entries.shape)]
        where[longest] = (where[longest] + shift) % entries.shape[longest]
        spots.append(tuple(where))
    return entries.at[spots[0]].set(least).at[spots[1]].set(largest)


def block_scale(rng, shape, pieces, smallest, largest):
    level = 1.0
    for position, shards_of in pieces:
        steps = jax.random.uniform(jax.random.fold_in(jax.random.fold_in(rng, 6), position), (shards_of,), jnp.float32, smallest / len(pieces), largest / len(pieces))
        level = level * jnp.repeat(jnp.exp(steps), shape[position] // shards_of).reshape((-1,) + (1,) * (len(shape) - 1 - position))
    return level


def scatter_about(key, extent, scale, limit, pieces=(), kind=jnp.bfloat16):
    loudness = block_scale(key, extent, pieces, -0.22, 0.18) if pieces else 1.0
    array = jax.random.normal(key, extent, jnp.float32) * scale * loudness
    return jnp.minimum(jnp.maximum(array, -limit), limit).astype(kind)


def setup_inputs(seed: int = 0) -> dict:
    seeds = jax.random.split(jax.random.key(seed), 9)
    return {
        "pivots": draw_pivots(jax.random.fold_in(seeds[8], 71), 0),
        "lower_spikes": draw_lower_spikes(jax.random.fold_in(seeds[8], 71), 0),
        "upper_spikes": draw_upper_spikes(jax.random.fold_in(seeds[8], 71), 0),
        "potential": scatter_about(seeds[3], (SLICES, B, B), B ** -0.5, 0.3125, ((0, 4), (1, 64)), jnp.float32),
        "grain_of_slice": place_ends(jax.random.randint(seeds[4], (SLICES,), 0, GRAINS), jax.random.fold_in(seeds[4], 1), 0, GRAINS - 1).astype(jnp.int32),
        "grain_shift": jnp.clip(jax.random.uniform(seeds[5], (GRAINS,), jnp.float32, 0.5, 1.5), 0.5, 1.5),
        "probes": scatter_about(seeds[6], (SLICES, B, PROBES), 1.0, 6.0, ((0, 4),), jnp.float32),
        "weights": jnp.clip(jnp.exp(math.log(2.0) - 1.3862944 * jax.random.uniform(seeds[7], (ENERGIES,), jnp.float32) ** block_scale(seeds[7], (ENERGIES,), ((0, 64),), -0.2, 0.2)), 0.5, 2.0),
    }


HIGHEST = lax.Precision.HIGHEST


def solve(pivot_blocks, lower_blocks, upper_blocks, right_side):
    solved_pivot = jnp.einsum("sij,sjk->sik", pivot_blocks, right_side, precision=HIGHEST)

    def advance(carried, inputs_pair):
        matrix_block, given_value = inputs_pair
        carried = given_value - jnp.dot(matrix_block, carried, precision=HIGHEST)
        return carried, carried

    zero_block = jnp.zeros(right_side.shape[1:], jnp.float32)
    _, climbed = lax.scan(advance, zero_block, (lower_blocks, solved_pivot))
    _, result = lax.scan(advance, zero_block, (upper_blocks, climbed), reverse=True)
    return result


def reference(pivots, lower_spikes, upper_spikes, potential, grain_of_slice, grain_shift, probes, weights):
    grain_match = grain_of_slice[:, None] == jnp.arange(GRAINS, dtype=jnp.int32)[None, :]
    grain_scale = jnp.sum(jnp.where(grain_match, grain_shift[None, :], 0.0), axis=1)
    perturb = potential * grain_scale[:, None, None]

    def per_energy(energy_inputs):
        pivot_blocks, lower_blocks, upper_blocks, weight = energy_inputs
        first_solve = solve(pivot_blocks, lower_blocks, upper_blocks, probes)
        driven = jnp.einsum("sij,sjk->sik", perturb, first_solve, precision=HIGHEST)
        second_solve = solve(pivot_blocks, lower_blocks, upper_blocks, driven)
        return weight * jnp.sum(second_solve * probes, axis=2)

    charge_terms = lax.map(per_energy, (pivots, lower_spikes, upper_spikes, weights))
    return jnp.sum(charge_terms, axis=0) / (PROBES * ENERGIES)
```

```python
import functools

import jax
import jax.numpy as jnp
from jax import lax
from jax.experimental import pallas as pl
from jax.experimental.pallas import tpu as pltpu
from jax.sharding import PartitionSpec as P

MESH = pl.DeviceIdType.MESH
F32 = jnp.float32
BF16 = jnp.bfloat16
CHUNKS = 2


def split(x):
    high = x.astype(BF16)
    low = (x - high.astype(F32)).astype(BF16)
    return high, low


def dot(a, b):
    return jnp.dot(a, b, preferred_element_type=F32)


def product(a_high, a_low, x):
    high, low = split(x)
    n = x.shape[1]
    both = dot(a_high, jnp.concatenate([high, low], axis=1))
    return (both[:, :n] + both[:, n:]) + dot(a_low, high)


def kernel(
    grain_ref, shift_ref, weight_ref, potential_ref, pivots, lower, upper, probes,
    out_ref,
    raw, z_ref, mat_h, mat_l, phi, w_h, w_l, psi_h, psi_l, x_ref, c_ref, y_in, x_in,
    gathered, message, landing, charge, part_a, part_b,
    load_sem, z_sem, chain_send, chain_recv, gat_send, gat_recv, red_send, red_recv,
):
    slices, orbitals, columns = z_ref.shape
    energies = lax.axis_size("energy")
    e = lax.axis_index("energy")
    d = lax.axis_index("dom")
    core = lax.rem(e, 2)
    zl = lax.rem(e // 2, 2)
    y = lax.rem(e // 4, 4)
    x = e // 16

    def at(xx, yy, zz, cc):
        return (((xx * 4 + yy) * 2 + zz) * 2 + cc, d)

    def off(value, by, size):
        return lax.rem(value + by, size)

    group_a = [(i, j) for i in range(4) for j in range(2) if i or j]

    def peer_a(i, j):
        return at(off(x, i, 4), y, zl, off(core, j, 2))

    def peer_b(i, j):
        return at(x, off(y, i, 4), off(zl, j, 2), core)

    def load(source, which, s):
        return pltpu.make_async_copy(
            source.at[0, s], raw.at[which * slices + s], load_sem.at[which * slices + s]
        )

    z_copy = pltpu.make_async_copy(probes, z_ref, z_sem)
    load(pivots, 0, 0).start()
    load(lower, 1, 0).start()
    z_copy.start()
    for s in range(1, slices):
        load(pivots, 0, s).start()
        load(lower, 1, s).start()
    for s in reversed(range(slices)):
        load(upper, 2, s).start()

    barrier = pltpu.get_barrier_semaphore()
    for i, j in group_a:
        pl.semaphore_signal(barrier, inc=1, device_id=peer_a(i, j), device_id_type=MESH)
        pl.semaphore_signal(barrier, inc=1, device_id=peer_b(i, j), device_id_type=MESH)

    @pl.when(d > 0)
    def _():
        pl.semaphore_signal(barrier, inc=1, device_id=(e, d - 1), device_id_type=MESH)

    @pl.when(d < 3)
    def _():
        pl.semaphore_signal(barrier, inc=1, device_id=(e, d + 1), device_id_type=MESH)

    for s in range(slices):
        scale = shift_ref[grain_ref[s]]
        own = potential_ref[s] * scale
        for r in range(5):
            for t in range(3):
                piece = own[r : r + 1, 128 * t : min(128 * t + 128, orbitals)]
                gathered[t, x, y, zl, core, r * 8 + s : r * 8 + s + 1, 0 : piece.shape[1]] = piece

    @pl.when(jnp.logical_or(d == 0, d == 3))
    def _():
        pl.semaphore_wait(barrier, 2 * len(group_a) + 1)

    @pl.when(jnp.logical_and(d > 0, d < 3))
    def _():
        pl.semaphore_wait(barrier, 2 * len(group_a) + 2)

    def gather_copy(ref, slot, device):
        return pltpu.make_async_remote_copy(
            src_ref=ref, dst_ref=ref, send_sem=gat_send.at[slot], recv_sem=gat_recv.at[slot],
            device_id=device, device_id_type=MESH,
        )

    def stage_1():
        return [gather_copy(gathered.at[:, x, y, zl, core], 0, at(x, y, off(zl, 1, 2), core))]

    def along_x(ref, base):
        return [gather_copy(ref, base + k, at(off(x, k, 4), y, zl, core)) for k in (1, 2, 3)]

    def along_y(ref, base):
        return [gather_copy(ref, base + k, at(x, off(y, k, 4), zl, core)) for k in (1, 2, 3)]

    def stage_2(first):
        ref = gathered.at[:, x, y, :, core]
        return along_x(ref, 0) if first else along_y(ref, 0)

    def stage_3(first):
        if first:
            return along_y(gathered.at[:, :, y, :, core], 3)
        return along_x(gathered.at[:, x, :, :, core], 3)

    def stage_4():
        return [gather_copy(gathered.at[:, :, :, :, core], 7, at(x, y, zl, off(core, 1, 2)))]

    def on_core(action):
        @pl.when(core == 0)
        def _():
            action(True)

        @pl.when(core == 1)
        def _():
            action(False)

    def start_2(first):
        for copy in stage_2(first):
            copy.start()

    def start_3(first):
        for copy in stage_2(first):
            copy.wait_recv()
        for copy in stage_3(first):
            copy.start()

    def end_3(first):
        for copy in stage_3(first):
            copy.wait_recv()

    def end_sends(first):
        for copy in stage_2(first) + stage_3(first):
            copy.wait_send()

    stage_1()[0].start()

    half = columns // 2
    rows = orbitals // 2
    left = lax.broadcasted_iota(jnp.int32, (rows, columns), 1) < half

    def turn(v):
        return pltpu.roll(v, half, 1)

    def pack(v):
        return jnp.where(left, v[:rows], turn(v[rows:]))

    def unpack(m):
        return jnp.concatenate([m, turn(m)], axis=0)

    def join(v0, v1):
        wide = lax.broadcasted_iota(jnp.int32, (orbitals, columns), 1) < half
        return jnp.where(wide, v0, turn(v1))

    def chain_copy(step, c, device):
        slot = step * CHUNKS + c
        return pltpu.make_async_remote_copy(
            src_ref=message.at[slot], dst_ref=landing.at[slot],
            send_sem=chain_send.at[slot], recv_sem=chain_recv.at[slot],
            device_id=device, device_id_type=MESH,
        )

    def emit(step, c, value, device):
        message[step * CHUNKS + c] = pack(value)
        chain_copy(step, c, device).start()

    def emit_all(step, value, device):
        emit(step, 0, value, device)
        emit(step, 1, turn(value), device)

    def receive(step, c):
        chain_copy(step, c, (e, d)).wait_recv()
        return unpack(landing[step * CHUNKS + c])

    def relay(step, own, high, low, device, keep):
        v0 = receive(step, 0)
        emit(step, 0, own + product(high, low, v0), device)
        v1 = receive(step, 1)
        emit(step, 1, turn(own) + product(high, low, v1), device)
        keep[...] = join(v0, v1)

    def take(step, keep):
        v0 = receive(step, 0)
        keep[...] = join(v0, receive(step, 1))

    up = (e, d + 1)
    down = (e, d - 1)
    last = slices - 1

    def matrix(which, s):
        return mat_h[which * slices + s], mat_l[which * slices + s]

    def keep_split(which, s):
        high, low = split(raw[which * slices + s])
        mat_h[which * slices + s] = high
        mat_l[which * slices + s] = low

    z_copy.wait()
    load(pivots, 0, 0).wait()
    load(lower, 1, 0).wait()
    keep_split(0, 0)
    keep_split(1, 0)
    c_ref[0] = product(*matrix(0, 0), z_ref[0])

    def climb_first(s, _):
        load(pivots, 0, s).wait()
        load(lower, 1, s).wait()
        keep_split(0, s)
        keep_split(1, s)
        c = product(*matrix(0, s), z_ref[s])
        c_ref[s] = c - product(*matrix(1, s), c_ref[s - 1])
        return 0

    lax.fori_loop(1, slices, climb_first, 0)

    @pl.when(d == 0)
    def _():
        emit_all(0, c_ref[last], up)

    stage_1()[0].wait_recv()
    on_core(start_2)

    phi[0] = -raw[slices]

    def grow(s, _):
        phi[s] = -product(*matrix(1, s), phi[s - 1])
        return 0

    lax.fori_loop(1, slices, grow, 0)
    f_high, f_low = mat_h.at[3 * slices], mat_l.at[3 * slices]
    high, low = split(phi[last])
    f_high[...] = high
    f_low[...] = low
    on_core(start_3)

    def forward_relay(step):
        relay(step, c_ref[last], f_high[...], f_low[...], up, y_in)

    @pl.when(d == 1)
    def _():
        forward_relay(0)

    load(upper, 2, last).wait()
    keep_split(2, last)
    x_ref[last] = c_ref[last]
    w_h[last], w_l[last] = split(phi[last])
    psi = -raw[2 * slices + last]
    psi_h[last], psi_l[last] = split(psi)

    def product_of_pairs(a_high, a_low, high, low):
        n = high.shape[1]
        both = dot(a_high, jnp.concatenate([high, low], axis=1))
        return (both[:, :n] + both[:, n:]) + dot(a_low, high)

    def descend_first(k, _):
        s = last - k
        load(upper, 2, s).wait()
        keep_split(2, s)
        u = matrix(2, s)
        x_ref[s] = c_ref[s] - product(*u, x_ref[s + 1])
        w_h[s], w_l[s] = split(phi[s] - product_of_pairs(*u, w_h[s + 1], w_l[s + 1]))
        psi_h[s], psi_l[s] = split(-product_of_pairs(*u, psi_h[s + 1], psi_l[s + 1]))
        return 0

    lax.fori_loop(1, 4, descend_first, 0)

    @pl.when(d == 2)
    def _():
        forward_relay(0)

    lax.fori_loop(4, slices, descend_first, 0)

    def middle(step):
        @pl.when(d == 3)
        def _():
            take(step, y_in)

        @pl.when(d > 0)
        def _():
            x_ref[0] = x_ref[0] + product(w_h[0], w_l[0], y_in[...])

        @pl.when(d == 3)
        def _():
            emit_all(step + 1, x_ref[0], down)

        @pl.when(d > 0)
        def _():
            def spread(s, _):
                x_ref[s] = x_ref[s] + product(w_h[s], w_l[s], y_in[...])
                return 0

            lax.fori_loop(1, slices, spread, 0)

        @pl.when(jnp.logical_or(d == 1, d == 2))
        def _():
            relay(step + 1, x_ref[0], psi_h[0], psi_l[0], down, x_in)

        @pl.when(d == 0)
        def _():
            take(step + 1, x_in)

        @pl.when(d == 3)
        def _():
            x_in[...] = jnp.zeros_like(x_in)

    middle(0)
    on_core(end_3)
    stage_4()[0].start()
    stage_4()[0].wait_recv()

    flat = gathered.reshape(3 * energies * 40, 128)

    def drive(s, _):
        value = x_ref[s] + product(psi_h[s], psi_l[s], x_in[...])
        tiles = [flat[pl.ds(t * energies * 40 + s, orbitals, stride=8), :] for t in range(3)]
        tiles[2] = tiles[2][:, : orbitals - 256]
        block_high, block_low = split(jnp.concatenate(tiles, axis=1))
        driven = product(block_high, block_low, value)
        c_ref[s] = product(*matrix(0, s), driven)
        return 0

    lax.fori_loop(0, slices, drive, 0)

    def climb(s, _):
        c_ref[s] = c_ref[s] - product(*matrix(1, s), c_ref[s - 1])
        return 0

    lax.fori_loop(1, slices, climb, 0)

    @pl.when(d == 0)
    def _():
        emit_all(2, c_ref[last], up)

    @pl.when(jnp.logical_or(d == 1, d == 2))
    def _():
        forward_relay(2)

    x_ref[last] = c_ref[last]

    def descend(k, _):
        s = last - k
        x_ref[s] = c_ref[s] - product(*matrix(2, s), x_ref[s + 1])
        return 0

    lax.fori_loop(1, slices, descend, 0)
    middle(2)

    ones = jnp.ones((8, columns), BF16)
    factor = weight_ref[0] / (columns * energies)
    dims = (((1,), (1,)), ((), ()))

    def finish(s, _):
        value = x_ref[s] + product(psi_h[s], psi_l[s], x_in[...])
        high, low = split(value * z_ref[s])
        total = lax.dot_general(ones, high, dims, preferred_element_type=F32)
        total = total + lax.dot_general(ones, low, dims, preferred_element_type=F32)
        charge[pl.ds(s, 1), 0:orbitals] = total[0:1] * factor
        return 0

    charge[...] = jnp.zeros_like(charge)
    lax.fori_loop(0, slices, finish, 0)

    def exchange(source, parts, base, peer):
        copies = [
            pltpu.make_async_remote_copy(
                src_ref=source, dst_ref=parts.at[n], send_sem=red_send.at[base + n],
                recv_sem=red_recv.at[base + n], device_id=peer(i, j), device_id_type=MESH,
            )
            for n, (i, j) in enumerate(group_a)
        ]
        for copy in copies:
            copy.start()
        total = source[...]
        for n, copy in enumerate(copies):
            copy.wait_recv()
            total = total + parts[n]
        return total, copies

    total, sent_a = exchange(charge, part_a, 0, peer_a)
    part_b[7] = total
    total, sent_b = exchange(part_b.at[7], part_b, 7, peer_b)
    total = pltpu.roll(total, lax.rem(384 - 5 * e, 384), 1)
    out_ref[...] = total[:, :5]

    for copy in sent_a + sent_b + stage_1() + stage_4():
        copy.wait_send()
    on_core(end_sends)

    def chain_end(steps, device):
        for step in steps:
            for c in range(CHUNKS):
                chain_copy(step, c, device).wait_send()

    @pl.when(d < 3)
    def _():
        chain_end((0, 2), up)

    @pl.when(d > 0)
    def _():
        chain_end((1, 3), down)


def per_device(
    pivots, lower_spikes, upper_spikes, potential, grain_of_slice, grain_shift, probes, weights
):
    slices, orbitals, columns = probes.shape
    smem = pl.BlockSpec(memory_space=pltpu.SMEM)
    vmem = pl.BlockSpec(memory_space=pltpu.VMEM)
    hbm = pl.BlockSpec(memory_space=pl.ANY)
    dma = pltpu.SemaphoreType.DMA
    square = (slices, orbitals, orbitals)
    wide = (slices, orbitals, columns)
    return pl.pallas_call(
        kernel,
        out_shape=jax.ShapeDtypeStruct((slices, 5), F32),
        in_specs=[smem, smem, smem, vmem, hbm, hbm, hbm, hbm],
        out_specs=vmem,
        scratch_shapes=[
            pltpu.VMEM((3 * slices, orbitals, orbitals), F32),
            pltpu.VMEM(wide, F32),
            pltpu.VMEM((3 * slices + 1, orbitals, orbitals), BF16),
            pltpu.VMEM((3 * slices + 1, orbitals, orbitals), BF16),
            pltpu.VMEM(square, F32),
            pltpu.VMEM(square, BF16),
            pltpu.VMEM(square, BF16),
            pltpu.VMEM(square, BF16),
            pltpu.VMEM(square, BF16),
            pltpu.VMEM(wide, F32),
            pltpu.VMEM(wide, F32),
            pltpu.VMEM((orbitals, columns), F32),
            pltpu.VMEM((orbitals, columns), F32),
            pltpu.VMEM((3, 4, 4, 2, 2, 40, 128), F32),
            pltpu.VMEM((4 * CHUNKS, orbitals // CHUNKS, columns), F32),
            pltpu.VMEM((4 * CHUNKS, orbitals // CHUNKS, columns), F32),
            pltpu.VMEM((slices, 384), F32),
            pltpu.VMEM((7, slices, 384), F32),
            pltpu.VMEM((8, slices, 384), F32),
            dma((3 * slices,)),
            dma,
            dma((4 * CHUNKS,)),
            dma((4 * CHUNKS,)),
            dma((8,)),
            dma((8,)),
            dma((14,)),
            dma((14,)),
        ],
        compiler_params=pltpu.CompilerParams(
            collective_id=0, has_side_effects=True, vmem_limit_bytes=60 * 1024 * 1024
        ),
    )(grain_of_slice, grain_shift, weights, potential, pivots, lower_spikes, upper_spikes, probes)


def solution(mesh):
    placed = (
        P("energy", "dom", None, None),
        P("energy", "dom", None, None),
        P("energy", "dom", None, None),
        P("dom", "energy", None),
        P("dom"),
        P(),
        P("dom", None, None),
        P("energy"),
    )
    return jax.shard_map(
        per_device, mesh=mesh, in_specs=placed, out_specs=P("dom", "energy"), check_vma=False
    )
```

```python
import functools

import jax
import jax.numpy as jnp
from jax import lax
from jax.experimental import pallas as pl
from jax.experimental.pallas import tpu as pltpu
from jax.sharding import PartitionSpec as P

MESH = pl.DeviceIdType.MESH
F32 = jnp.float32
BF16 = jnp.bfloat16
CHUNKS = 2


def split(x):
    high = x.astype(BF16)
    low = (x - high.astype(F32)).astype(BF16)
    return high, low


def dot(a, b):
    return jnp.dot(a, b, preferred_element_type=F32)


def product(a_high, a_low, x):
    high, low = split(x)
    n = x.shape[1]
    both = dot(a_high, jnp.concatenate([high, low], axis=1))
    return (both[:, :n] + both[:, n:]) + dot(a_low, high)


def kernel(
    grain_ref, shift_ref, weight_ref, potential, pivots, lower, upper, probes,
    out_ref,
    potential_ref, reflect,
    raw, z_ref, mat_h, mat_l, phi, w_h, w_l, psi_h, psi_l, x_ref, c_ref, y_in, x_in,
    gathered, message, landing, charge, part_a, part_b,
    load_sem, z_sem, chain_send, chain_recv, gat_send, gat_recv, red_send, red_recv, pot_sem, mat_send, mat_recv,
):
    slices, orbitals, columns = z_ref.shape
    energies = lax.axis_size("energy")
    e = lax.axis_index("energy")
    d = lax.axis_index("dom")
    core = lax.rem(e, 2)
    zl = lax.rem(e // 2, 2)
    y = lax.rem(e // 4, 4)
    x = e // 16

    def at(xx, yy, zz, cc):
        return (((xx * 4 + yy) * 2 + zz) * 2 + cc, d)

    def off(value, by, size):
        return lax.rem(value + by, size)

    group_a = [(i, j) for i in range(4) for j in range(2) if i or j]

    def peer_a(i, j):
        return at(off(x, i, 4), y, zl, off(core, j, 2))

    def peer_b(i, j):
        return at(x, off(y, i, 4), off(zl, j, 2), core)

    def load(source, which, s):
        return pltpu.make_async_copy(
            source.at[0, s], raw.at[which * slices + s], load_sem.at[which * slices + s]
        )

    z_copy = pltpu.make_async_copy(probes, z_ref, z_sem)
    pot_copy = pltpu.make_async_copy(potential, potential_ref, pot_sem)
    pot_copy.start()
    load(pivots, 0, 0).start()
    load(lower, 1, 0).start()
    z_copy.start()
    for s in range(1, slices):
        load(pivots, 0, s).start()
        load(lower, 1, s).start()
    for s in reversed(range(slices)):
        load(upper, 2, s).start()

    barrier = pltpu.get_barrier_semaphore()
    for i, j in group_a:
        pl.semaphore_signal(barrier, inc=1, device_id=peer_a(i, j), device_id_type=MESH)
        pl.semaphore_signal(barrier, inc=1, device_id=peer_b(i, j), device_id_type=MESH)

    @pl.when(d > 0)
    def _():
        pl.semaphore_signal(barrier, inc=1, device_id=(e, d - 1), device_id_type=MESH)

    @pl.when(d < 3)
    def _():
        pl.semaphore_signal(barrier, inc=1, device_id=(e, d + 1), device_id_type=MESH)

    pot_copy.wait()
    for s in range(slices):
        scale = shift_ref[grain_ref[s]]
        own = potential_ref[s] * scale
        for r in range(5):
            for t in range(3):
                piece = own[r : r + 1, 128 * t : min(128 * t + 128, orbitals)]
                gathered[t, x, y, zl, core, r * 8 + s : r * 8 + s + 1, 0 : piece.shape[1]] = piece

    @pl.when(jnp.logical_or(d == 0, d == 3))
    def _():
        pl.semaphore_wait(barrier, 2 * len(group_a) + 1)

    @pl.when(jnp.logical_and(d > 0, d < 3))
    def _():
        pl.semaphore_wait(barrier, 2 * len(group_a) + 2)

    def gather_copy(ref, slot, device):
        return pltpu.make_async_remote_copy(
            src_ref=ref, dst_ref=ref, send_sem=gat_send.at[slot], recv_sem=gat_recv.at[slot],
            device_id=device, device_id_type=MESH,
        )

    def stage_1():
        return [gather_copy(gathered.at[:, x, y, zl, core], 0, at(x, y, off(zl, 1, 2), core))]

    def along_x(ref, base):
        return [gather_copy(ref, base + k, at(off(x, k, 4), y, zl, core)) for k in (1, 2, 3)]

    def along_y(ref, base):
        return [gather_copy(ref, base + k, at(x, off(y, k, 4), zl, core)) for k in (1, 2, 3)]

    def stage_2(first):
        ref = gathered.at[:, x, y, :, core]
        return along_x(ref, 0) if first else along_y(ref, 0)

    def stage_3(first):
        if first:
            return along_y(gathered.at[:, :, y, :, core], 3)
        return along_x(gathered.at[:, x, :, :, core], 3)

    def stage_4():
        return [gather_copy(gathered.at[:, :, :, :, core], 7, at(x, y, zl, off(core, 1, 2)))]

    def on_core(action):
        @pl.when(core == 0)
        def _():
            action(True)

        @pl.when(core == 1)
        def _():
            action(False)

    def start_2(first):
        for copy in stage_2(first):
            copy.start()

    def start_3(first):
        for copy in stage_2(first):
            copy.wait_recv()
        for copy in stage_3(first):
            copy.start()

    def end_3(first):
        for copy in stage_3(first):
            copy.wait_recv()

    def end_sends(first):
        for copy in stage_2(first) + stage_3(first):
            copy.wait_send()

    stage_1()[0].start()

    half = columns // 2
    rows = orbitals // 2
    left = lax.broadcasted_iota(jnp.int32, (rows, columns), 1) < half

    def turn(v):
        return pltpu.roll(v, half, 1)

    def pack(v):
        return jnp.where(left, v[:rows], turn(v[rows:]))

    def unpack(m):
        return jnp.concatenate([m, turn(m)], axis=0)

    def join(v0, v1):
        wide = lax.broadcasted_iota(jnp.int32, (orbitals, columns), 1) < half
        return jnp.where(wide, v0, turn(v1))

    def chain_copy(step, c, device):
        slot = step * CHUNKS + c
        return pltpu.make_async_remote_copy(
            src_ref=message.at[slot], dst_ref=landing.at[slot],
            send_sem=chain_send.at[slot], recv_sem=chain_recv.at[slot],
            device_id=device, device_id_type=MESH,
        )

    def emit(step, c, value, device):
        message[step * CHUNKS + c] = pack(value)
        chain_copy(step, c, device).start()

    def emit_all(step, value, device):
        emit(step, 0, value, device)
        emit(step, 1, turn(value), device)

    def receive(step, c):
        chain_copy(step, c, (e, d)).wait_recv()
        return unpack(landing[step * CHUNKS + c])

    def relay(step, own, high, low, device, keep):
        v0 = receive(step, 0)
        emit(step, 0, own + product(high, low, v0), device)
        v1 = receive(step, 1)
        emit(step, 1, turn(own) + product(high, low, v1), device)
        keep[...] = join(v0, v1)

    def take(step, keep):
        v0 = receive(step, 0)
        keep[...] = join(v0, receive(step, 1))

    up = (e, d + 1)
    down = (e, d - 1)
    last = slices - 1

    def matrix(which, s):
        return mat_h[which * slices + s], mat_l[which * slices + s]

    def keep_split(which, s):
        high, low = split(raw[which * slices + s])
        mat_h[which * slices + s] = high
        mat_l[which * slices + s] = low

    def loop(first, end, action, unroll=1):
        lax.fori_loop(first, end, lambda s, carry: (action(s), carry)[1], 0, unroll=unroll)

    def perturbation(s):
        tiles = [flat[pl.ds(t * energies * 40 + s, orbitals, stride=8), :] for t in range(3)]
        tiles[2] = tiles[2][:, : orbitals - 256]
        return jnp.concatenate(tiles, axis=1)

    flat = gathered.reshape(3 * energies * 40, 128)

    def product_of_pairs(a_high, a_low, high, low):
        n = high.shape[1]
        both = dot(a_high, jnp.concatenate([high, low], axis=1))
        return (both[:, :n] + both[:, n:]) + dot(a_low, high)

    def is_dom(*which):
        test = d == which[0]
        for w in which[1:]:
            test = jnp.logical_or(test, d == w)
        return pl.when(test)

    z_copy.wait()
    load(pivots, 0, 0).wait()
    load(lower, 1, 0).wait()
    keep_split(0, 0)
    keep_split(1, 0)
    c_ref[0] = product(*matrix(0, 0), z_ref[0])

    def climb_first(s):
        load(pivots, 0, s).wait()
        load(lower, 1, s).wait()
        keep_split(0, s)
        keep_split(1, s)
        c = product(*matrix(0, s), z_ref[s])
        c_ref[s] = c - product(*matrix(1, s), c_ref[s - 1])

    loop(1, 5, climb_first)
    stage_1()[0].wait_recv()
    on_core(start_2)
    loop(5, slices, climb_first)

    f_high, f_low = mat_h.at[3 * slices], mat_l.at[3 * slices]

    def grow(s):
        phi[s] = -product(*matrix(1, s), phi[s - 1])

    def forward_relay(step):
        relay(step, c_ref[last], f_high[...], f_low[...], up, y_in)

    def descend_values(s):
        x_ref[s] = c_ref[s] - product(*matrix(2, s), x_ref[s + 1])

    def descend_w(s):
        w_h[s], w_l[s] = split(phi[s] - product_of_pairs(*matrix(2, s), w_h[s + 1], w_l[s + 1]))

    def descend_psi(s):
        psi_h[s], psi_l[s] = split(-product_of_pairs(*matrix(2, s), psi_h[s + 1], psi_l[s + 1]))

    def fetch_upper(s):
        load(upper, 2, s).wait()
        keep_split(2, s)

    def descend_first(with_w, with_psi):
        def action(k):
            s = last - k
            fetch_upper(s)
            descend_values(s)
            if with_w:
                descend_w(s)
            if with_psi:
                descend_psi(s)

        return action

    @is_dom(0)
    def _():
        emit_all(0, c_ref[last], up)

    @is_dom(1, 2, 3)
    def _():
        phi[0] = -raw[slices]
        loop(1, slices, grow)
        w_h[last], w_l[last] = split(phi[last])
        f_high[...] = w_h[last]
        f_low[...] = w_l[last]

    @is_dom(1)
    def _():
        forward_relay(0)

    on_core(start_3)
    fetch_upper(last)
    x_ref[last] = c_ref[last]
    psi_h[last], psi_l[last] = split(-raw[2 * slices + last])

    @is_dom(0)
    def _():
        loop(1, slices, descend_first(False, True))

    @is_dom(1)
    def _():
        loop(1, slices, descend_first(True, True))

    @is_dom(2)
    def _():
        loop(1, 4, descend_first(True, True))
        forward_relay(0)
        loop(4, slices, descend_first(True, True))

    @is_dom(3)
    def _():
        loop(1, slices, descend_first(True, False))

    def add_inflow(s):
        x_ref[s] = x_ref[s] + product(w_h[s], w_l[s], y_in[...])

    def end_gather():
        on_core(end_3)
        stage_4()[0].start()
        stage_4()[0].wait_recv()

    def reflect_copy(device):
        return pltpu.make_async_remote_copy(
            src_ref=phi.at[0], dst_ref=reflect, send_sem=mat_send, recv_sem=mat_recv,
            device_id=device, device_id_type=MESH,
        )

    def backward_relay(step):
        relay(step, x_ref[0], psi_h[0], psi_l[0], down, x_in)

    @is_dom(3)
    def _():
        take(0, y_in)
        add_inflow(0)
        emit_all(1, x_ref[0], down)
        phi[0] = w_h[0].astype(F32) + w_l[0].astype(F32)
        reflect_copy(down).start()
        loop(1, slices, add_inflow, 7)
        x_in[...] = jnp.zeros_like(x_in)
        end_gather()

    @is_dom(2)
    def _():
        loop(0, slices, add_inflow, 4)
        backward_relay(1)
        end_gather()

    @is_dom(1)
    def _():
        loop(0, slices, add_inflow, 4)
        end_gather()
        backward_relay(1)

    @is_dom(0)
    def _():
        end_gather()
        f_high[...] = jnp.zeros_like(f_high)
        f_low[...] = jnp.zeros_like(f_low)
        y_in[...] = jnp.zeros_like(y_in)

        def fold(s):
            joint = split(product_of_pairs(*matrix(0, s), *split(perturbation(s))))
            given = product(*joint, x_ref[s])
            reply = product_of_pairs(*joint, psi_h[s], psi_l[s])
            y_in[...] = given - product(*matrix(1, s), y_in[...])
            f_high[...], f_low[...] = split(
                reply - product_of_pairs(*matrix(1, s), f_high[...], f_low[...])
            )

        loop(0, slices, fold)
        v0 = receive(1, 0)
        emit(2, 0, y_in[...] + product(f_high[...], f_low[...], v0), up)
        v1 = receive(1, 1)
        emit(2, 1, turn(y_in[...]) + product(f_high[...], f_low[...], v1), up)
        x_in[...] = join(v0, v1)

    def drive(s):
        value = x_ref[s] + product(psi_h[s], psi_l[s], x_in[...])
        driven = product(*split(perturbation(s)), value)
        c_ref[s] = product(*matrix(0, s), driven)

    def drive_last(s):
        driven = product(*split(perturbation(s)), x_ref[s])
        c_ref[s] = product(*matrix(0, s), driven)

    @is_dom(0, 1, 2)
    def _():
        loop(0, slices, drive, 4)

    @is_dom(3)
    def _():
        loop(0, slices, drive_last, 4)

    def climb(s):
        c_ref[s] = c_ref[s] - product(*matrix(1, s), c_ref[s - 1])

    loop(1, slices, climb)

    @is_dom(1)
    def _():
        forward_relay(2)

    x_ref[last] = c_ref[last]
    loop(1, slices, lambda k: descend_values(last - k))

    @is_dom(3)
    def _():
        emit_all(3, x_ref[0], down)
        take(2, y_in)
        loop(0, slices, add_inflow, 4)

    @is_dom(2)
    def _():
        reflect_copy((e, d)).wait_recv()
        beyond = split(reflect[...])
        answer = product(psi_h[0], psi_l[0], product_of_pairs(*beyond, f_high[...], f_low[...]))
        answer = split(answer + (w_h[0].astype(F32) + w_l[0].astype(F32)))
        take(3, x_in)
        x_in[...] = x_in[...] + product(*beyond, c_ref[last])
        own = x_ref[0] + product(psi_h[0], psi_l[0], x_in[...])
        v0 = receive(2, 0)
        emit(3, 0, own + product(*answer, v0), down)
        v1 = receive(2, 1)
        emit(3, 1, turn(own) + product(*answer, v1), down)
        out0 = product(f_high[...], f_low[...], v0)
        emit(2, 0, c_ref[last] + out0, up)
        out1 = product(f_high[...], f_low[...], v1)
        emit(2, 1, turn(c_ref[last]) + out1, up)
        y_in[...] = join(v0, v1)
        x_in[...] = x_in[...] + product(*beyond, join(out0, out1))
        loop(0, slices, add_inflow, 4)

    @is_dom(1)
    def _():
        loop(0, slices, add_inflow, 4)
        backward_relay(3)

    @is_dom(0)
    def _():
        take(3, x_in)

    ones = jnp.ones((8, columns), BF16)
    factor = weight_ref[0] / (columns * energies)
    dims = (((1,), (1,)), ((), ()))

    def finish(s):
        value = x_ref[s] + product(psi_h[s], psi_l[s], x_in[...])
        high, low = split(value * z_ref[s])
        total = lax.dot_general(ones, high, dims, preferred_element_type=F32)
        total = total + lax.dot_general(ones, low, dims, preferred_element_type=F32)
        charge[pl.ds(s, 1), 0:orbitals] = total[0:1] * factor

    charge[...] = jnp.zeros_like(charge)
    loop(0, slices, finish, 4)

    def exchange(source, parts, base, peer):
        copies = [
            pltpu.make_async_remote_copy(
                src_ref=source, dst_ref=parts.at[n], send_sem=red_send.at[base + n],
                recv_sem=red_recv.at[base + n], device_id=peer(i, j), device_id_type=MESH,
            )
            for n, (i, j) in enumerate(group_a)
        ]
        for copy in copies:
            copy.start()
        total = source[...]
        for n, copy in enumerate(copies):
            copy.wait_recv()
            total = total + parts[n]
        return total, copies

    total, sent_a = exchange(charge, part_a, 0, peer_a)
    part_b[7] = total
    total, sent_b = exchange(part_b.at[7], part_b, 7, peer_b)
    total = pltpu.roll(total, lax.rem(384 - 5 * e, 384), 1)
    out_ref[...] = total[:, :5]

    for copy in sent_a + sent_b + stage_1() + stage_4():
        copy.wait_send()
    on_core(end_sends)

    def chain_end(steps, device):
        for step in steps:
            for c in range(CHUNKS):
                chain_copy(step, c, device).wait_send()

    @pl.when(d < 3)
    def _():
        chain_end((0, 2), up)

    @pl.when(d > 0)
    def _():
        chain_end((1, 3), down)

    @is_dom(3)
    def _():
        reflect_copy(down).wait_send()


def per_device(
    pivots, lower_spikes, upper_spikes, potential, grain_of_slice, grain_shift, probes, weights
):
    slices, orbitals, columns = probes.shape
    smem = pl.BlockSpec(memory_space=pltpu.SMEM)
    vmem = pl.BlockSpec(memory_space=pltpu.VMEM)
    hbm = pl.BlockSpec(memory_space=pl.ANY)
    dma = pltpu.SemaphoreType.DMA
    square = (slices, orbitals, orbitals)
    wide = (slices, orbitals, columns)
    return pl.pallas_call(
        kernel,
        out_shape=jax.ShapeDtypeStruct((slices, 5), F32),
        in_specs=[smem, smem, smem, hbm, hbm, hbm, hbm, hbm],
        out_specs=vmem,
        scratch_shapes=[
            pltpu.VMEM((slices, 5, orbitals), F32),
            pltpu.VMEM((orbitals, orbitals), F32),
            pltpu.VMEM((3 * slices, orbitals, orbitals), F32),
            pltpu.VMEM(wide, F32),
            pltpu.VMEM((3 * slices + 1, orbitals, orbitals), BF16),
            pltpu.VMEM((3 * slices + 1, orbitals, orbitals), BF16),
            pltpu.VMEM(square, F32),
            pltpu.VMEM(square, BF16),
            pltpu.VMEM(square, BF16),
            pltpu.VMEM(square, BF16),
            pltpu.VMEM(square, BF16),
            pltpu.VMEM(wide, F32),
            pltpu.VMEM(wide, F32),
            pltpu.VMEM((orbitals, columns), F32),
            pltpu.VMEM((orbitals, columns), F32),
            pltpu.VMEM((3, 4, 4, 2, 2, 40, 128), F32),
            pltpu.VMEM((4 * CHUNKS, orbitals // CHUNKS, columns), F32),
            pltpu.VMEM((4 * CHUNKS, orbitals // CHUNKS, columns), F32),
            pltpu.VMEM((slices, 384), F32),
            pltpu.VMEM((7, slices, 384), F32),
            pltpu.VMEM((8, slices, 384), F32),
            dma((3 * slices,)),
            dma,
            dma((4 * CHUNKS,)),
            dma((4 * CHUNKS,)),
            dma((8,)),
            dma((8,)),
            dma((14,)),
            dma((14,)),
            dma,
            dma,
            dma,
        ],
        compiler_params=pltpu.CompilerParams(
            collective_id=0, has_side_effects=True, vmem_limit_bytes=60 * 1024 * 1024
        ),
    )(grain_of_slice, grain_shift, weights, potential, pivots, lower_spikes, upper_spikes, probes)


def solution(mesh):
    placed = (
        P("energy", "dom", None, None),
        P("energy", "dom", None, None),
        P("energy", "dom", None, None),
        P("dom", "energy", None),
        P("dom"),
        P(),
        P("dom", None, None),
        P("energy"),
    )
    return jax.shard_map(
        per_device, mesh=mesh, in_specs=placed, out_specs=P("dom", "energy"), check_vma=False
    )
```

```python
import functools

import jax
import jax.numpy as jnp
from jax import lax
from jax.experimental import pallas as pl
from jax.experimental.pallas import tpu as pltpu
from jax.sharding import PartitionSpec as P

MESH = pl.DeviceIdType.MESH
F32 = jnp.float32
BF16 = jnp.bfloat16
CHUNKS = 2


def split(x):
    high = x.astype(BF16)
    low = (x - high.astype(F32)).astype(BF16)
    return high, low


def dot(a, b):
    return jnp.dot(a, b, preferred_element_type=F32)


def product(a_high, a_low, x):
    high, low = split(x)
    n = x.shape[1]
    both = dot(a_high, jnp.concatenate([high, low], axis=1))
    return (both[:, :n] + both[:, n:]) + dot(a_low, high)


def kernel(
    grain_ref, shift_ref, weight_ref, potential, pivots, lower, upper, probes,
    out_ref,
    potential_ref, reflect_out, reflect,
    raw, z_ref, mat_h, mat_l, phi, w_h, w_l, psi_h, psi_l, x_ref, c_ref, y_in, x_in,
    gathered, message, landing, charge, part_a, part_b,
    load_sem, z_sem, chain_send, chain_recv, gat_send, gat_recv, red_send, red_recv, pot_sem, mat_send, mat_recv,
):
    slices, orbitals, columns = z_ref.shape
    energies = lax.axis_size("energy")
    e = lax.axis_index("energy")
    d = lax.axis_index("dom")
    core = lax.rem(e, 2)
    zl = lax.rem(e // 2, 2)
    y = lax.rem(e // 4, 4)
    x = e // 16

    def at(xx, yy, zz, cc):
        return (((xx * 4 + yy) * 2 + zz) * 2 + cc, d)

    def off(value, by, size):
        return lax.rem(value + by, size)

    group_a = [(i, j) for i in range(4) for j in range(2) if i or j]

    def peer_a(i, j):
        return at(off(x, i, 4), y, zl, off(core, j, 2))

    def peer_b(i, j):
        return at(x, off(y, i, 4), off(zl, j, 2), core)

    def load(source, which, s):
        return pltpu.make_async_copy(
            source.at[0, s], raw.at[which * slices + s], load_sem.at[which * slices + s]
        )

    z_copy = pltpu.make_async_copy(probes, z_ref, z_sem)
    pot_copy = pltpu.make_async_copy(potential, potential_ref, pot_sem)
    pot_copy.start()
    load(pivots, 0, 0).start()
    load(lower, 1, 0).start()
    z_copy.start()
    for s in range(1, slices):
        load(pivots, 0, s).start()
        load(lower, 1, s).start()
    for s in reversed(range(slices)):
        load(upper, 2, s).start()

    barrier = pltpu.get_barrier_semaphore()
    for i, j in group_a:
        pl.semaphore_signal(barrier, inc=1, device_id=peer_a(i, j), device_id_type=MESH)
        pl.semaphore_signal(barrier, inc=1, device_id=peer_b(i, j), device_id_type=MESH)

    @pl.when(d > 0)
    def _():
        pl.semaphore_signal(barrier, inc=1, device_id=(e, d - 1), device_id_type=MESH)

    @pl.when(d < 3)
    def _():
        pl.semaphore_signal(barrier, inc=1, device_id=(e, d + 1), device_id_type=MESH)

    pot_copy.wait()
    for s in range(slices):
        scale = shift_ref[grain_ref[s]]
        own = potential_ref[s] * scale
        for r in range(5):
            for t in range(3):
                piece = own[r : r + 1, 128 * t : min(128 * t + 128, orbitals)]
                gathered[t, x, y, zl, core, r * 8 + s : r * 8 + s + 1, 0 : piece.shape[1]] = piece

    def gather_copy(ref, slot, device):
        return pltpu.make_async_remote_copy(
            src_ref=ref, dst_ref=ref, send_sem=gat_send.at[slot], recv_sem=gat_recv.at[slot],
            device_id=device, device_id_type=MESH,
        )

    def stage_1():
        return [gather_copy(gathered.at[:, x, y, zl, core], 0, at(x, y, off(zl, 1, 2), core))]

    def block(first, k):
        if first:
            return gathered.at[:, off(x, 4 - k, 4), y, :, core]
        return gathered.at[:, x, off(y, 4 - k, 4), :, core]

    def line(first, k):
        if first:
            return gathered.at[:, :, off(y, 4 - k, 4), :, core]
        return gathered.at[:, off(x, 4 - k, 4), :, :, core]

    def ahead(along_x, k):
        if along_x:
            return at(off(x, k, 4), y, zl, core)
        return at(x, off(y, k, 4), zl, core)

    def stage_2(first, k):
        return gather_copy(block(first, 0), k, ahead(first, k))

    def stage_3(first, j, k):
        return gather_copy(block(first, j), 4 * k + j, ahead(not first, k))

    def stage_4(first, k):
        return gather_copy(line(first, k), 16 + k, at(x, y, zl, off(core, 1, 2)))

    def on_core(action):
        @pl.when(core == 0)
        def _():
            action(True)

        @pl.when(core == 1)
        def _():
            action(False)

    def forward_block(first, j):
        for k in (1, 3, 2):
            stage_3(first, j, k).start()

    def start_2(first):
        for k in (1, 3, 2):
            stage_2(first, k).start()
        forward_block(first, 0)

    def start_3(first):
        for j in (1, 3, 2):
            stage_2(first, j).wait_recv()
            forward_block(first, j)
        stage_4(first, 0).start()

    def end_3(first):
        for k in (1, 3, 2):
            for j in range(4):
                stage_3(first, j, k).wait_recv()
            stage_4(first, k).start()
        for k in range(4):
            stage_4(first, k).wait_recv()

    def end_sends(first):
        for k in (1, 2, 3):
            stage_2(first, k).wait_send()
            for j in range(4):
                stage_3(first, j, k).wait_send()
        for k in range(4):
            stage_4(first, k).wait_send()

    def gather_1():
        stage_1()[0].wait_recv()
        on_core(start_2)

    def gather_2():
        on_core(start_3)

    def end_gather():
        on_core(end_3)

    half = columns // 2
    rows = orbitals // 2
    left = lax.broadcasted_iota(jnp.int32, (rows, columns), 1) < half

    def turn(v):
        return pltpu.roll(v, half, 1)

    def pack(v):
        return jnp.where(left, v[:rows], turn(v[rows:]))

    def unpack(m):
        return jnp.concatenate([m, turn(m)], axis=0)

    def join(v0, v1):
        wide = lax.broadcasted_iota(jnp.int32, (orbitals, columns), 1) < half
        return jnp.where(wide, v0, turn(v1))

    def chain_copy(step, c, device):
        slot = step * CHUNKS + c
        return pltpu.make_async_remote_copy(
            src_ref=message.at[slot], dst_ref=landing.at[slot],
            send_sem=chain_send.at[slot], recv_sem=chain_recv.at[slot],
            device_id=device, device_id_type=MESH,
        )

    def emit(step, c, value, device):
        message[step * CHUNKS + c] = pack(value)
        chain_copy(step, c, device).start()

    def emit_all(step, value, device):
        emit(step, 0, value, device)
        emit(step, 1, turn(value), device)

    def receive(step, c):
        chain_copy(step, c, (e, d)).wait_recv()
        return unpack(landing[step * CHUNKS + c])

    def relay(step, own, high, low, device, keep):
        v0 = receive(step, 0)
        emit(step, 0, own + product(high, low, v0), device)
        v1 = receive(step, 1)
        emit(step, 1, turn(own) + product(high, low, v1), device)
        keep[...] = join(v0, v1)

    def take(step, keep):
        v0 = receive(step, 0)
        keep[...] = join(v0, receive(step, 1))

    up = (e, d + 1)
    down = (e, d - 1)
    last = slices - 1

    def matrix(which, s):
        return mat_h[which * slices + s], mat_l[which * slices + s]

    def keep_split(which, s):
        high, low = split(raw[which * slices + s])
        mat_h[which * slices + s] = high
        mat_l[which * slices + s] = low

    def loop(first, end, action, unroll=1):
        lax.fori_loop(first, end, lambda s, carry: (action(s), carry)[1], 0, unroll=unroll)

    def perturbation(s):
        tiles = [flat[pl.ds(t * energies * 40 + s, orbitals, stride=8), :] for t in range(3)]
        tiles[2] = tiles[2][:, : orbitals - 256]
        return jnp.concatenate(tiles, axis=1)

    flat = gathered.reshape(3 * energies * 40, 128)

    def product_of_pairs(a_high, a_low, high, low):
        n = high.shape[1]
        both = dot(a_high, jnp.concatenate([high, low], axis=1))
        return (both[:, :n] + both[:, n:]) + dot(a_low, high)

    def is_dom(*which):
        test = d == which[0]
        for w in which[1:]:
            test = jnp.logical_or(test, d == w)
        return pl.when(test)

    z_copy.wait()
    load(pivots, 0, 0).wait()
    load(lower, 1, 0).wait()
    keep_split(0, 0)
    keep_split(1, 0)
    c_ref[0] = product(*matrix(0, 0), z_ref[0])

    def climb_first(s):
        load(pivots, 0, s).wait()
        load(lower, 1, s).wait()
        keep_split(0, s)
        keep_split(1, s)
        c = product(*matrix(0, s), z_ref[s])
        c_ref[s] = c - product(*matrix(1, s), c_ref[s - 1])

    loop(1, 4, climb_first)
    @pl.when(jnp.logical_or(d == 0, d == 3))
    def _():
        pl.semaphore_wait(barrier, 2 * len(group_a) + 1)

    @pl.when(jnp.logical_and(d > 0, d < 3))
    def _():
        pl.semaphore_wait(barrier, 2 * len(group_a) + 2)

    stage_1()[0].start()
    loop(4, slices, climb_first)

    f_high, f_low = mat_h.at[3 * slices], mat_l.at[3 * slices]

    def grow(s):
        phi[s] = -product(*matrix(1, s), phi[s - 1])

    def forward_relay(step):
        relay(step, c_ref[last], f_high[...], f_low[...], up, y_in)

    def descend_values(s):
        x_ref[s] = c_ref[s] - product(*matrix(2, s), x_ref[s + 1])

    def descend_w(s):
        w_h[s], w_l[s] = split(phi[s] - product_of_pairs(*matrix(2, s), w_h[s + 1], w_l[s + 1]))

    def descend_psi(s):
        psi_h[s], psi_l[s] = split(-product_of_pairs(*matrix(2, s), psi_h[s + 1], psi_l[s + 1]))

    def fetch_upper(s):
        load(upper, 2, s).wait()
        keep_split(2, s)

    def descend_first(with_w, with_psi):
        def action(k):
            s = last - k
            fetch_upper(s)
            descend_values(s)
            if with_w:
                descend_w(s)
            if with_psi:
                descend_psi(s)

        return action

    @is_dom(0)
    def _():
        emit_all(0, c_ref[last], up)
        gather_1()

    @is_dom(1, 2, 3)
    def _():
        phi[0] = -raw[slices]
        loop(1, 4, grow)
        gather_1()
        loop(4, slices, grow)
        w_h[last], w_l[last] = split(phi[last])
        f_high[...] = w_h[last]
        f_low[...] = w_l[last]

    @is_dom(1)
    def _():
        forward_relay(0)

    fetch_upper(last)
    x_ref[last] = c_ref[last]
    psi_h[last], psi_l[last] = split(-raw[2 * slices + last])

    @is_dom(0)
    def _():
        loop(1, 5, descend_first(False, True))
        gather_2()
        loop(5, slices, descend_first(False, True))

    @is_dom(1)
    def _():
        gather_2()
        loop(1, slices, descend_first(True, True))

    @is_dom(2)
    def _():
        loop(1, 3, descend_first(True, True))
        gather_2()
        loop(3, 4, descend_first(True, True))
        forward_relay(0)
        loop(4, slices, descend_first(True, True))

    @is_dom(3)
    def _():
        loop(1, 4, descend_first(True, False))
        gather_2()
        loop(4, slices, descend_first(True, False))

    def add_inflow(s):
        x_ref[s] = x_ref[s] + product(w_h[s], w_l[s], y_in[...])

    def reflect_copy(device):
        return pltpu.make_async_remote_copy(
            src_ref=reflect_out, dst_ref=reflect, send_sem=mat_send, recv_sem=mat_recv,
            device_id=device, device_id_type=MESH,
        )

    def backward_relay(step):
        relay(step, x_ref[0], psi_h[0], psi_l[0], down, x_in)

    @is_dom(3)
    def _():
        w = w_h[0], w_l[0]
        v0 = receive(0, 0)
        emit(1, 0, x_ref[0] + product(*w, v0), down)
        v1 = receive(0, 1)
        emit(1, 1, turn(x_ref[0]) + product(*w, v1), down)
        y_in[...] = join(v0, v1)
        whole = w_h[0].astype(F32) + w_l[0].astype(F32)
        reflect_out[:orbitals] = whole[:, :columns]
        reflect_out[orbitals : 2 * orbitals] = whole[:, columns : 2 * columns]
        rest = jnp.concatenate([whole[:, 2 * columns :], jnp.zeros((orbitals, half), F32)], axis=1)
        reflect_out[2 * orbitals :] = pack(rest)
        reflect_copy(down).start()
        loop(0, slices, add_inflow, 4)
        x_in[...] = jnp.zeros_like(x_in)
        end_gather()

    @is_dom(2)
    def _():
        loop(0, slices, add_inflow, 4)
        backward_relay(1)
        end_gather()

    @is_dom(1)
    def _():
        loop(0, slices, add_inflow, 4)
        backward_relay(1)
        end_gather()

    @is_dom(0)
    def _():
        end_gather()
        f_high[...] = jnp.zeros_like(f_high)
        f_low[...] = jnp.zeros_like(f_low)
        y_in[...] = jnp.zeros_like(y_in)

        def fold(s):
            joint = split(product_of_pairs(*matrix(0, s), *split(perturbation(s))))
            given = product(*joint, x_ref[s])
            reply = product_of_pairs(*joint, psi_h[s], psi_l[s])
            y_in[...] = given - product(*matrix(1, s), y_in[...])
            f_high[...], f_low[...] = split(
                reply - product_of_pairs(*matrix(1, s), f_high[...], f_low[...])
            )

        loop(0, slices, fold, 2)
        v0 = receive(1, 0)
        emit(2, 0, y_in[...] + product(f_high[...], f_low[...], v0), up)
        v1 = receive(1, 1)
        emit(2, 1, turn(y_in[...]) + product(f_high[...], f_low[...], v1), up)
        x_in[...] = join(v0, v1)

    def drive(s):
        value = x_ref[s] + product(psi_h[s], psi_l[s], x_in[...])
        driven = product(*split(perturbation(s)), value)
        c_ref[s] = product(*matrix(0, s), driven)

    def drive_last(s):
        driven = product(*split(perturbation(s)), x_ref[s])
        c_ref[s] = product(*matrix(0, s), driven)

    @is_dom(0, 1, 2)
    def _():
        loop(0, slices, drive, 4)

    @is_dom(3)
    def _():
        loop(0, slices, drive_last, 4)

    def climb(s):
        c_ref[s] = c_ref[s] - product(*matrix(1, s), c_ref[s - 1])

    loop(1, slices, climb)

    @is_dom(1)
    def _():
        forward_relay(2)

    x_ref[last] = c_ref[last]
    loop(1, slices, lambda k: descend_values(last - k))

    @is_dom(3)
    def _():
        emit_all(3, x_ref[0], down)
        take(2, y_in)
        loop(0, slices, add_inflow, 4)

    @is_dom(2)
    def _():
        reflect_copy((e, d)).wait_recv()
        rest = unpack(reflect[2 * orbitals :])[:, :half]
        whole = [reflect[:orbitals], reflect[orbitals : 2 * orbitals], rest]
        beyond = split(jnp.concatenate(whole, axis=1))
        answer = product(psi_h[0], psi_l[0], product_of_pairs(*beyond, f_high[...], f_low[...]))
        answer = split(answer + (w_h[0].astype(F32) + w_l[0].astype(F32)))
        take(3, x_in)
        x_in[...] = x_in[...] + product(*beyond, c_ref[last])
        own = x_ref[0] + product(psi_h[0], psi_l[0], x_in[...])
        v0 = receive(2, 0)
        emit(3, 0, own + product(*answer, v0), down)
        v1 = receive(2, 1)
        emit(3, 1, turn(own) + product(*answer, v1), down)
        out0 = product(f_high[...], f_low[...], v0)
        emit(2, 0, c_ref[last] + out0, up)
        out1 = product(f_high[...], f_low[...], v1)
        emit(2, 1, turn(c_ref[last]) + out1, up)
        y_in[...] = join(v0, v1)
        x_in[...] = x_in[...] + product(*beyond, join(out0, out1))
        loop(0, slices, add_inflow, 4)

    @is_dom(1)
    def _():
        loop(0, slices, add_inflow, 4)
        backward_relay(3)

    @is_dom(0)
    def _():
        take(3, x_in)

    ones = jnp.ones((8, columns), BF16)
    factor = weight_ref[0] / (columns * energies)
    dims = (((1,), (1,)), ((), ()))

    def finish(s):
        value = x_ref[s] + product(psi_h[s], psi_l[s], x_in[...])
        high, low = split(value * z_ref[s])
        total = lax.dot_general(ones, high, dims, preferred_element_type=F32)
        total = total + lax.dot_general(ones, low, dims, preferred_element_type=F32)
        charge[pl.ds(s, 1), 0:orbitals] = total[0:1] * factor

    charge[...] = jnp.zeros_like(charge)
    loop(0, slices, finish, 4)

    def exchange(source, parts, base, peer):
        copies = [
            pltpu.make_async_remote_copy(
                src_ref=source, dst_ref=parts.at[n], send_sem=red_send.at[base + n],
                recv_sem=red_recv.at[base + n], device_id=peer(i, j), device_id_type=MESH,
            )
            for n, (i, j) in enumerate(group_a)
        ]
        for copy in copies:
            copy.start()
        total = source[...]
        for n, copy in enumerate(copies):
            copy.wait_recv()
            total = total + parts[n]
        return total, copies

    total, sent_a = exchange(charge, part_a, 0, peer_a)
    part_b[7] = total
    total, sent_b = exchange(part_b.at[7], part_b, 7, peer_b)
    total = pltpu.roll(total, lax.rem(384 - 5 * e, 384), 1)
    out_ref[...] = total[:, :5]

    for copy in sent_a + sent_b + stage_1():
        copy.wait_send()
    on_core(end_sends)

    def chain_end(steps, device):
        for step in steps:
            for c in range(CHUNKS):
                chain_copy(step, c, device).wait_send()

    @pl.when(d < 3)
    def _():
        chain_end((0, 2), up)

    @pl.when(d > 0)
    def _():
        chain_end((1, 3), down)

    @is_dom(3)
    def _():
        reflect_copy(down).wait_send()


def per_device(
    pivots, lower_spikes, upper_spikes, potential, grain_of_slice, grain_shift, probes, weights
):
    slices, orbitals, columns = probes.shape
    smem = pl.BlockSpec(memory_space=pltpu.SMEM)
    vmem = pl.BlockSpec(memory_space=pltpu.VMEM)
    hbm = pl.BlockSpec(memory_space=pl.ANY)
    dma = pltpu.SemaphoreType.DMA
    square = (slices, orbitals, orbitals)
    wide = (slices, orbitals, columns)
    return pl.pallas_call(
        kernel,
        out_shape=jax.ShapeDtypeStruct((slices, 5), F32),
        in_specs=[smem, smem, smem, hbm, hbm, hbm, hbm, hbm],
        out_specs=vmem,
        scratch_shapes=[
            pltpu.VMEM((slices, 5, orbitals), F32),
            pltpu.VMEM((5 * orbitals // 2, columns), F32),
            pltpu.VMEM((5 * orbitals // 2, columns), F32),
            pltpu.VMEM((3 * slices, orbitals, orbitals), F32),
            pltpu.VMEM(wide, F32),
            pltpu.VMEM((3 * slices + 1, orbitals, orbitals), BF16),
            pltpu.VMEM((3 * slices + 1, orbitals, orbitals), BF16),
            pltpu.VMEM(square, F32),
            pltpu.VMEM(square, BF16),
            pltpu.VMEM(square, BF16),
            pltpu.VMEM(square, BF16),
            pltpu.VMEM(square, BF16),
            pltpu.VMEM(wide, F32),
            pltpu.VMEM(wide, F32),
            pltpu.VMEM((orbitals, columns), F32),
            pltpu.VMEM((orbitals, columns), F32),
            pltpu.VMEM((3, 4, 4, 2, 2, 40, 128), F32),
            pltpu.VMEM((4 * CHUNKS, orbitals // CHUNKS, columns), F32),
            pltpu.VMEM((4 * CHUNKS, orbitals // CHUNKS, columns), F32),
            pltpu.VMEM((slices, 384), F32),
            pltpu.VMEM((7, slices, 384), F32),
            pltpu.VMEM((8, slices, 384), F32),
            dma((3 * slices,)),
            dma,
            dma((4 * CHUNKS,)),
            dma((4 * CHUNKS,)),
            dma((20,)),
            dma((20,)),
            dma((14,)),
            dma((14,)),
            dma,
            dma,
            dma,
        ],
        compiler_params=pltpu.CompilerParams(
            collective_id=0, has_side_effects=True, vmem_limit_bytes=60 * 1024 * 1024
        ),
    )(grain_of_slice, grain_shift, weights, potential, pivots, lower_spikes, upper_spikes, probes)


def solution(mesh):
    placed = (
        P("energy", "dom", None, None),
        P("energy", "dom", None, None),
        P("energy", "dom", None, None),
        P("dom", "energy", None),
        P("dom"),
        P(),
        P("dom", None, None),
        P("energy"),
    )
    return jax.shard_map(
        per_device, mesh=mesh, in_specs=placed, out_specs=P("dom", "energy"), check_vma=False
    )
```

```python
import functools

import jax
import jax.numpy as jnp
from jax import lax
from jax.experimental import pallas as pl
from jax.experimental.pallas import tpu as pltpu
from jax.sharding import PartitionSpec as P

MESH = pl.DeviceIdType.MESH
F32 = jnp.float32
BF16 = jnp.bfloat16
CHUNKS = 2


def split(x):
    high = x.astype(BF16)
    low = (x - high.astype(F32)).astype(BF16)
    return high, low


def dot(a, b):
    return jnp.dot(a, b, preferred_element_type=F32)


def product(a_high, a_low, x):
    high, low = split(x)
    n = x.shape[1]
    both = dot(a_high, jnp.concatenate([high, low], axis=1))
    return (both[:, :n] + both[:, n:]) + dot(a_low, high)


def kernel(
    grain_ref, shift_ref, weight_ref, potential, pivots, lower, upper, probes,
    out_ref,
    potential_ref, reflect_out, reflect,
    raw, z_ref, mat_h, mat_l, phi, w_h, w_l, psi_h, psi_l, x_ref, c_ref, y_in, x_in,
    gathered, message, landing, charge, part_a, part_b,
    load_sem, z_sem, chain_send, chain_recv, gat_send, gat_recv, red_send, red_recv, pot_sem, mat_send, mat_recv,
):
    slices, orbitals, columns = z_ref.shape
    energies = lax.axis_size("energy")
    e = lax.axis_index("energy")
    d = lax.axis_index("dom")
    core = lax.rem(e, 2)
    zl = lax.rem(e // 2, 2)
    y = lax.rem(e // 4, 4)
    x = e // 16

    def at(xx, yy, zz, cc):
        return (((xx * 4 + yy) * 2 + zz) * 2 + cc, d)

    def off(value, by, size):
        return lax.rem(value + by, size)

    group_a = [(i, j) for i in range(4) for j in range(2) if i or j]

    def peer_a(i, j):
        return at(off(x, i, 4), y, zl, off(core, j, 2))

    def peer_b(i, j):
        return at(x, off(y, i, 4), off(zl, j, 2), core)

    def load(source, which, s):
        return pltpu.make_async_copy(
            source.at[0, s], raw.at[which * slices + s], load_sem.at[which * slices + s]
        )

    z_copy = pltpu.make_async_copy(probes, z_ref, z_sem)
    pot_copy = pltpu.make_async_copy(potential, potential_ref, pot_sem)
    pot_copy.start()
    load(pivots, 0, 0).start()
    load(lower, 1, 0).start()
    z_copy.start()
    for s in range(1, slices):
        load(pivots, 0, s).start()
        load(lower, 1, s).start()
    for s in reversed(range(slices)):
        load(upper, 2, s).start()

    barrier = pltpu.get_barrier_semaphore()
    for i, j in group_a:
        pl.semaphore_signal(barrier, inc=1, device_id=peer_a(i, j), device_id_type=MESH)
        pl.semaphore_signal(barrier, inc=1, device_id=peer_b(i, j), device_id_type=MESH)

    @pl.when(d > 0)
    def _():
        pl.semaphore_signal(barrier, inc=1, device_id=(e, d - 1), device_id_type=MESH)

    @pl.when(d < 3)
    def _():
        pl.semaphore_signal(barrier, inc=1, device_id=(e, d + 1), device_id_type=MESH)

    pot_copy.wait()
    for s in range(slices):
        scale = shift_ref[grain_ref[s]]
        own = potential_ref[s] * scale
        for r in range(5):
            for t in range(3):
                piece = own[r : r + 1, 128 * t : min(128 * t + 128, orbitals)]
                gathered[t, x, y, zl, core, r * 8 + s : r * 8 + s + 1, 0 : piece.shape[1]] = piece

    def gather_copy(ref, slot, device):
        return pltpu.make_async_remote_copy(
            src_ref=ref, dst_ref=ref, send_sem=gat_send.at[slot], recv_sem=gat_recv.at[slot],
            device_id=device, device_id_type=MESH,
        )

    def stage_1():
        return [gather_copy(gathered.at[:, x, y, zl, core], 0, at(x, y, off(zl, 1, 2), core))]

    def block(first, k):
        if first:
            return gathered.at[:, off(x, 4 - k, 4), y, :, core]
        return gathered.at[:, x, off(y, 4 - k, 4), :, core]

    def line(first, k):
        if first:
            return gathered.at[:, :, off(y, 4 - k, 4), :, core]
        return gathered.at[:, off(x, 4 - k, 4), :, :, core]

    def ahead(along_x, k):
        if along_x:
            return at(off(x, k, 4), y, zl, core)
        return at(x, off(y, k, 4), zl, core)

    def stage_2(first, k):
        return gather_copy(block(first, 0), k, ahead(first, k))

    def stage_3(first, j, k):
        return gather_copy(block(first, j), 4 * k + j, ahead(not first, k))

    def stage_4(first, k):
        return gather_copy(line(first, k), 16 + k, at(x, y, zl, off(core, 1, 2)))

    def on_core(action):
        @pl.when(core == 0)
        def _():
            action(True)

        @pl.when(core == 1)
        def _():
            action(False)

    def forward_block(first, j):
        for k in (1, 3, 2):
            stage_3(first, j, k).start()

    def start_2(first):
        for k in (1, 3, 2):
            stage_2(first, k).start()
        forward_block(first, 0)

    def start_3(first):
        for j in (1, 3, 2):
            stage_2(first, j).wait_recv()
            forward_block(first, j)
        stage_4(first, 0).start()

    def end_3(first):
        for k in (1, 3, 2):
            for j in range(4):
                stage_3(first, j, k).wait_recv()
            stage_4(first, k).start()
        for k in range(4):
            stage_4(first, k).wait_recv()

    def end_sends(first):
        for k in (1, 2, 3):
            stage_2(first, k).wait_send()
            for j in range(4):
                stage_3(first, j, k).wait_send()
        for k in range(4):
            stage_4(first, k).wait_send()

    def gather_1():
        stage_1()[0].wait_recv()
        on_core(start_2)

    def gather_2():
        on_core(start_3)

    def end_gather():
        on_core(end_3)

    half = columns // 2
    rows = orbitals // 2
    left = lax.broadcasted_iota(jnp.int32, (rows, columns), 1) < half

    def turn(v):
        return pltpu.roll(v, half, 1)

    def pack(v):
        return jnp.where(left, v[:rows], turn(v[rows:]))

    def unpack(m):
        return jnp.concatenate([m, turn(m)], axis=0)

    def join(v0, v1):
        wide = lax.broadcasted_iota(jnp.int32, (orbitals, columns), 1) < half
        return jnp.where(wide, v0, turn(v1))

    def chain_copy(step, c, device):
        slot = step * CHUNKS + c
        return pltpu.make_async_remote_copy(
            src_ref=message.at[slot], dst_ref=landing.at[slot],
            send_sem=chain_send.at[slot], recv_sem=chain_recv.at[slot],
            device_id=device, device_id_type=MESH,
        )

    def emit(step, c, value, device):
        message[step * CHUNKS + c] = pack(value)
        chain_copy(step, c, device).start()

    def emit_all(step, value, device):
        emit(step, 0, value, device)
        emit(step, 1, turn(value), device)

    def receive(step, c):
        chain_copy(step, c, (e, d)).wait_recv()
        return unpack(landing[step * CHUNKS + c])

    def relay(step, own, high, low, device, keep):
        v0 = receive(step, 0)
        emit(step, 0, own + product(high, low, v0), device)
        v1 = receive(step, 1)
        emit(step, 1, turn(own) + product(high, low, v1), device)
        keep[...] = join(v0, v1)

    def take(step, keep):
        v0 = receive(step, 0)
        keep[...] = join(v0, receive(step, 1))

    up = (e, d + 1)
    down = (e, d - 1)
    last = slices - 1

    def matrix(which, s):
        return mat_h[which * slices + s], mat_l[which * slices + s]

    def keep_split(which, s):
        high, low = split(raw[which * slices + s])
        mat_h[which * slices + s] = high
        mat_l[which * slices + s] = low

    def loop(first, end, action, unroll=1):
        lax.fori_loop(first, end, lambda s, carry: (action(s), carry)[1], 0, unroll=unroll)

    def perturbation(s):
        tiles = [flat[pl.ds(t * energies * 40 + s, orbitals, stride=8), :] for t in range(3)]
        tiles[2] = tiles[2][:, : orbitals - 256]
        return jnp.concatenate(tiles, axis=1)

    flat = gathered.reshape(3 * energies * 40, 128)

    def product_of_pairs(a_high, a_low, high, low):
        n = high.shape[1]
        both = dot(a_high, jnp.concatenate([high, low], axis=1))
        return (both[:, :n] + both[:, n:]) + dot(a_low, high)

    def is_dom(*which):
        test = d == which[0]
        for w in which[1:]:
            test = jnp.logical_or(test, d == w)
        return pl.when(test)

    z_copy.wait()
    load(pivots, 0, 0).wait()
    load(lower, 1, 0).wait()
    keep_split(0, 0)
    keep_split(1, 0)
    c_ref[0] = product(*matrix(0, 0), z_ref[0])

    def climb_first(s):
        load(pivots, 0, s).wait()
        load(lower, 1, s).wait()
        keep_split(0, s)
        keep_split(1, s)
        c = product(*matrix(0, s), z_ref[s])
        c_ref[s] = c - product(*matrix(1, s), c_ref[s - 1])

    loop(1, 4, climb_first)
    @pl.when(jnp.logical_or(d == 0, d == 3))
    def _():
        pl.semaphore_wait(barrier, 2 * len(group_a) + 1)

    @pl.when(jnp.logical_and(d > 0, d < 3))
    def _():
        pl.semaphore_wait(barrier, 2 * len(group_a) + 2)

    stage_1()[0].start()
    loop(4, slices, climb_first)

    f_high, f_low = mat_h.at[3 * slices], mat_l.at[3 * slices]

    def grow(s):
        phi[s] = -product(*matrix(1, s), phi[s - 1])

    def forward_relay(step):
        relay(step, c_ref[last], f_high[...], f_low[...], up, y_in)

    def descend_values(s):
        x_ref[s] = c_ref[s] - product(*matrix(2, s), x_ref[s + 1])

    def descend_w(s):
        w_h[s], w_l[s] = split(phi[s] - product_of_pairs(*matrix(2, s), w_h[s + 1], w_l[s + 1]))

    def descend_psi(s):
        psi_h[s], psi_l[s] = split(-product_of_pairs(*matrix(2, s), psi_h[s + 1], psi_l[s + 1]))

    def fetch_upper(s):
        load(upper, 2, s).wait()
        keep_split(2, s)

    def descend_first(with_w, with_psi):
        def action(k):
            s = last - k
            fetch_upper(s)
            descend_values(s)
            if with_w:
                descend_w(s)
            if with_psi:
                descend_psi(s)

        return action

    @is_dom(0)
    def _():
        emit_all(0, c_ref[last], up)
        gather_1()

    @is_dom(1, 2, 3)
    def _():
        phi[0] = -raw[slices]
        loop(1, 4, grow)
        gather_1()
        loop(4, slices, grow)
        w_h[last], w_l[last] = split(phi[last])
        f_high[...] = w_h[last]
        f_low[...] = w_l[last]

    @is_dom(1)
    def _():
        forward_relay(0)

    fetch_upper(last)
    x_ref[last] = c_ref[last]
    psi_h[last], psi_l[last] = split(-raw[2 * slices + last])

    @is_dom(0)
    def _():
        loop(1, 5, descend_first(False, True))
        gather_2()
        loop(5, slices, descend_first(False, True))

    @is_dom(1)
    def _():
        gather_2()
        loop(1, slices, descend_first(True, True))

    @is_dom(2)
    def _():
        loop(1, 3, descend_first(True, True))
        gather_2()
        loop(3, 4, descend_first(True, True))
        forward_relay(0)
        loop(4, slices, descend_first(True, True))

    @is_dom(3)
    def _():
        loop(1, 4, descend_first(True, False))
        gather_2()
        loop(4, slices, descend_first(True, False))

    def add_inflow(s):
        x_ref[s] = x_ref[s] + product(w_h[s], w_l[s], y_in[...])

    def reflect_copy(device):
        return pltpu.make_async_remote_copy(
            src_ref=reflect_out, dst_ref=reflect, send_sem=mat_send, recv_sem=mat_recv,
            device_id=device, device_id_type=MESH,
        )

    def backward_relay(step):
        relay(step, x_ref[0], psi_h[0], psi_l[0], down, x_in)

    @is_dom(3)
    def _():
        w = w_h[0], w_l[0]
        v0 = receive(0, 0)
        emit(1, 0, x_ref[0] + product(*w, v0), down)
        v1 = receive(0, 1)
        emit(1, 1, turn(x_ref[0]) + product(*w, v1), down)
        y_in[...] = join(v0, v1)
        loop(0, slices, add_inflow, 4)
        x_in[...] = jnp.zeros_like(x_in)
        whole = w_h[0].astype(F32) + w_l[0].astype(F32)
        reflect_out[:orbitals] = whole[:, :columns]
        reflect_out[orbitals : 2 * orbitals] = whole[:, columns : 2 * columns]
        rest = jnp.concatenate([whole[:, 2 * columns :], jnp.zeros((orbitals, half), F32)], axis=1)
        reflect_out[2 * orbitals :] = pack(rest)
        reflect_copy(down).start()
        end_gather()

    @is_dom(2)
    def _():
        loop(0, slices, add_inflow, 4)
        backward_relay(1)
        end_gather()

    @is_dom(1)
    def _():
        loop(0, slices, add_inflow, 4)
        backward_relay(1)
        end_gather()

    @is_dom(0)
    def _():
        end_gather()
        f_high[...] = jnp.zeros_like(f_high)
        f_low[...] = jnp.zeros_like(f_low)
        y_in[...] = jnp.zeros_like(y_in)

        def fold(s):
            joint = split(product_of_pairs(*matrix(0, s), *split(perturbation(s))))
            given = product(*joint, x_ref[s])
            reply = product_of_pairs(*joint, psi_h[s], psi_l[s])
            y_in[...] = given - product(*matrix(1, s), y_in[...])
            f_high[...], f_low[...] = split(
                reply - product_of_pairs(*matrix(1, s), f_high[...], f_low[...])
            )

        loop(0, slices, fold, 2)
        v0 = receive(1, 0)
        emit(2, 0, y_in[...] + product(f_high[...], f_low[...], v0), up)
        v1 = receive(1, 1)
        emit(2, 1, turn(y_in[...]) + product(f_high[...], f_low[...], v1), up)
        x_in[...] = join(v0, v1)

    def drive(s):
        value = x_ref[s] + product(psi_h[s], psi_l[s], x_in[...])
        driven = product(*split(perturbation(s)), value)
        c_ref[s] = product(*matrix(0, s), driven)

    def drive_last(s):
        driven = product(*split(perturbation(s)), x_ref[s])
        c_ref[s] = product(*matrix(0, s), driven)

    @is_dom(0, 1, 2)
    def _():
        loop(0, slices, drive, 4)

    @is_dom(3)
    def _():
        loop(0, slices, drive_last, 4)

    def climb(s):
        c_ref[s] = c_ref[s] - product(*matrix(1, s), c_ref[s - 1])

    loop(1, slices, climb)

    @is_dom(1)
    def _():
        forward_relay(2)

    x_ref[last] = c_ref[last]
    loop(1, slices, lambda k: descend_values(last - k))

    @is_dom(3)
    def _():
        emit_all(3, x_ref[0], down)
        take(2, y_in)
        loop(0, slices, add_inflow, 4)

    @is_dom(2)
    def _():
        reflect_copy((e, d)).wait_recv()
        rest = unpack(reflect[2 * orbitals :])[:, :half]
        whole = [reflect[:orbitals], reflect[orbitals : 2 * orbitals], rest]
        beyond = split(jnp.concatenate(whole, axis=1))
        answer = product(psi_h[0], psi_l[0], product_of_pairs(*beyond, f_high[...], f_low[...]))
        answer = split(answer + (w_h[0].astype(F32) + w_l[0].astype(F32)))
        take(3, x_in)
        x_in[...] = x_in[...] + product(*beyond, c_ref[last])
        own = x_ref[0] + product(psi_h[0], psi_l[0], x_in[...])
        v0 = receive(2, 0)
        emit(3, 0, own + product(*answer, v0), down)
        v1 = receive(2, 1)
        emit(3, 1, turn(own) + product(*answer, v1), down)
        out0 = product(f_high[...], f_low[...], v0)
        emit(2, 0, c_ref[last] + out0, up)
        out1 = product(f_high[...], f_low[...], v1)
        emit(2, 1, turn(c_ref[last]) + out1, up)
        y_in[...] = join(v0, v1)
        x_in[...] = x_in[...] + product(*beyond, join(out0, out1))
        loop(0, slices, add_inflow, 4)

    @is_dom(1)
    def _():
        loop(0, slices, add_inflow, 4)
        backward_relay(3)

    @is_dom(0)
    def _():
        take(3, x_in)

    ones = jnp.ones((8, columns), BF16)
    factor = weight_ref[0] / (columns * energies)
    dims = (((1,), (1,)), ((), ()))

    def finish(s):
        value = x_ref[s] + product(psi_h[s], psi_l[s], x_in[...])
        high, low = split(value * z_ref[s])
        total = lax.dot_general(ones, high, dims, preferred_element_type=F32)
        total = total + lax.dot_general(ones, low, dims, preferred_element_type=F32)
        charge[pl.ds(s, 1), 0:orbitals] = total[0:1] * factor

    charge[...] = jnp.zeros_like(charge)
    loop(0, slices, finish, 4)

    def exchange(source, parts, base, peer):
        copies = [
            pltpu.make_async_remote_copy(
                src_ref=source, dst_ref=parts.at[n], send_sem=red_send.at[base + n],
                recv_sem=red_recv.at[base + n], device_id=peer(i, j), device_id_type=MESH,
            )
            for n, (i, j) in enumerate(group_a)
        ]
        for copy in copies:
            copy.start()
        total = source[...]
        for n, copy in enumerate(copies):
            copy.wait_recv()
            total = total + parts[n]
        return total, copies

    total, sent_a = exchange(charge, part_a, 0, peer_a)
    part_b[7] = total
    total, sent_b = exchange(part_b.at[7], part_b, 7, peer_b)
    total = pltpu.roll(total, lax.rem(384 - 5 * e, 384), 1)
    out_ref[...] = total[:, :5]

    for copy in sent_a + sent_b + stage_1():
        copy.wait_send()
    on_core(end_sends)

    def chain_end(steps, device):
        for step in steps:
            for c in range(CHUNKS):
                chain_copy(step, c, device).wait_send()

    @pl.when(d < 3)
    def _():
        chain_end((0, 2), up)

    @pl.when(d > 0)
    def _():
        chain_end((1, 3), down)

    @is_dom(3)
    def _():
        reflect_copy(down).wait_send()


def per_device(
    pivots, lower_spikes, upper_spikes, potential, grain_of_slice, grain_shift, probes, weights
):
    slices, orbitals, columns = probes.shape
    smem = pl.BlockSpec(memory_space=pltpu.SMEM)
    vmem = pl.BlockSpec(memory_space=pltpu.VMEM)
    hbm = pl.BlockSpec(memory_space=pl.ANY)
    dma = pltpu.SemaphoreType.DMA
    square = (slices, orbitals, orbitals)
    wide = (slices, orbitals, columns)
    return pl.pallas_call(
        kernel,
        out_shape=jax.ShapeDtypeStruct((slices, 5), F32),
        in_specs=[smem, smem, smem, hbm, hbm, hbm, hbm, hbm],
        out_specs=vmem,
        scratch_shapes=[
            pltpu.VMEM((slices, 5, orbitals), F32),
            pltpu.VMEM((5 * orbitals // 2, columns), F32),
            pltpu.VMEM((5 * orbitals // 2, columns), F32),
            pltpu.VMEM((3 * slices, orbitals, orbitals), F32),
            pltpu.VMEM(wide, F32),
            pltpu.VMEM((3 * slices + 1, orbitals, orbitals), BF16),
            pltpu.VMEM((3 * slices + 1, orbitals, orbitals), BF16),
            pltpu.VMEM(square, F32),
            pltpu.VMEM(square, BF16),
            pltpu.VMEM(square, BF16),
            pltpu.VMEM(square, BF16),
            pltpu.VMEM(square, BF16),
            pltpu.VMEM(wide, F32),
            pltpu.VMEM(wide, F32),
            pltpu.VMEM((orbitals, columns), F32),
            pltpu.VMEM((orbitals, columns), F32),
            pltpu.VMEM((3, 4, 4, 2, 2, 40, 128), F32),
            pltpu.VMEM((4 * CHUNKS, orbitals // CHUNKS, columns), F32),
            pltpu.VMEM((4 * CHUNKS, orbitals // CHUNKS, columns), F32),
            pltpu.VMEM((slices, 384), F32),
            pltpu.VMEM((7, slices, 384), F32),
            pltpu.VMEM((8, slices, 384), F32),
            dma((3 * slices,)),
            dma,
            dma((4 * CHUNKS,)),
            dma((4 * CHUNKS,)),
            dma((20,)),
            dma((20,)),
            dma((14,)),
            dma((14,)),
            dma,
            dma,
            dma,
        ],
        compiler_params=pltpu.CompilerParams(
            collective_id=0, has_side_effects=True, vmem_limit_bytes=60 * 1024 * 1024
        ),
    )(grain_of_slice, grain_shift, weights, potential, pivots, lower_spikes, upper_spikes, probes)


def solution(mesh):
    placed = (
        P("energy", "dom", None, None),
        P("energy", "dom", None, None),
        P("energy", "dom", None, None),
        P("dom", "energy", None),
        P("dom"),
        P(),
        P("dom", None, None),
        P("energy"),
    )
    return jax.shard_map(
        per_device, mesh=mesh, in_specs=placed, out_specs=P("dom", "energy"), check_vma=False
    )
```
